32 devices in a mesh: mem: 8 (over y, x, core), grid: 4 (over z).
Axes of the slice: x: 2, y: 2, z: 4, core: 2. Of those that a mesh axis runs over, the one named last changes fastest.
Arguments:
- ensemble: bfloat16 [16, 4, 128, 8, 128], P('mem', None, None, 'grid'), may hold values from -6 to 6
- control: bfloat16 [16, 128, 8, 128], P('mem', None, 'grid'), may hold values from -6 to 6
- vertical: bfloat16 [128, 128], replicated, may hold values from -0.5 to 0.5
- inverse_var: float32 [4, 128], replicated, may hold values from 0.25 to 4
- obs_code: int32 [16, 256], P('grid'), may hold values from 0 to 4
- obs_count: int32 [16, 256], P('grid'), may hold values from 0 to 3
Outputs:
- product: float32 [16, 128, 8, 128], P('mem', None, 'grid')
The draws below stay inside these ranges and needn't reach their ends.
All inputs are finite; a program needn't handle non-finite values.
Results may differ from the reference program's by a relative error of at most 0.00045.
Values sent between devices are 32-bit elements; how exact they have to be, the bound alone decides.
A program may use at most 64 MiB of HBM per device.

```python
import math
import jax
import jax.numpy as jnp
from jax import lax

VARS = 4
LEV = 128
CY = 128
MEMBERS = 16
NX = 8


def place_ends(array, key, least, largest):
    dims = array.shape
    place = [jax.random.randint(jax.random.fold_in(key, axis), (), 0, dims[axis]) for axis in range(len(dims))]
    array = array.at[tuple(place)].set(least)
    longest = dims.index(max(dims))
    place[longest] = (place[longest] + 1) % dims[longest]
    return array.at[tuple(place)].set(largest)


def spiked(values, rng, source, target, blocks, factor):
    def block_of(axis_at):
        return (jnp.arange(values.shape[axis_at]) // (values.shape[axis_at] // blocks)).reshape((-1,) + (1,) * (values.ndim - 1 - axis_at))

    one_side = jax.random.permutation(rng, blocks)[block_of(target)]
    far = (block_of(target) + blocks // 2) % blocks
    return jnp.where((block_of(source) == one_side) | (block_of(source) == far), factor * values, values)


def block_scale(own_key, extent, cuts, smallest, top_value):
    def one(axis_at, blocks):
        heights = jax.random.uniform(jax.random.fold_in(jax.random.fold_in(own_key, 6), axis_at), (blocks,), jnp.float32, smallest / len(cuts), top_value / len(cuts))
        return jnp.repeat(jnp.exp(heights), extent[axis_at] // blocks).reshape((-1,) + (1,) * (len(extent) - axis_at - 1))

    level = one(*cuts[0])
    for cut in cuts[1:]:
        level = level * one(*cut)
    return level


def centred(own_key, extent, deviation, bound, pieces=(), dtype=jnp.bfloat16):
    array = deviation * jax.random.normal(own_key, extent, jnp.float32)
    if pieces:
        array = array * block_scale(own_key, extent, pieces, -0.22, 0.18)
    return jnp.clip(array, -bound, bound).astype(dtype)


def noise_with(key, dims, scale, reach, pieces, heavy, dtype=jnp.bfloat16):
    entries = scale * jax.random.normal(key, dims, jnp.float32)
    if pieces:
        entries = entries * block_scale(key, dims, pieces, -0.22, 0.18)
    return jnp.clip(spiked(entries, jax.random.fold_in(key, 3), *heavy), -reach, reach).astype(dtype)


def setup_inputs(seed: int = 0) -> dict:
    key_list = jax.random.split(jax.random.key(seed), 7)
    ensemble = noise_with(key_list[0], (MEMBERS, VARS, LEV, NX, CY), 1.0, 6.0, ((0, 8), (3, 4)), (0, 2, 8, 2.0))
    control = centred(key_list[1], (MEMBERS, LEV, NX, CY), 1.0, 6.0, ((0, 8), (2, 4)))
    vertical = centred(key_list[2], (LEV, LEV), LEV ** -0.5, 0.5)
    inverse_var = jnp.clip(jnp.exp(jax.random.uniform(key_list[3], (VARS, LEV), jnp.float32, math.log(0.25), math.log(4.0))), 0.25, 4.0)
    obs_code = place_ends(jax.random.randint(key_list[4], (2 * NX, 2 * CY), 0, 5), jax.random.fold_in(key_list[4], 1), 0, 4).astype(jnp.int32)
    obs_count = place_ends(jax.random.randint(key_list[5], (2 * NX, 2 * CY), 0, 4), jax.random.fold_in(key_list[5], 1), 0, 3).astype(jnp.int32)
    return dict(ensemble=ensemble, control=control, vertical=vertical, inverse_var=inverse_var, obs_code=obs_code, obs_count=obs_count)


diffusion = 0.2
near_weight = 0.75
far_weight = 0.25


def column_pair(field):
    padded = jnp.pad(field, [(0, 0)] * (field.ndim - 1) + [(1, 1)])
    return padded[..., 2:] + padded[..., :-2]


def row_margin(field):
    return jnp.pad(field, [(0, 0)] * (field.ndim - 2) + [(1, 1), (0, 0)])


def smooth_rows(extended):
    center = extended[..., 1:-1, :]
    return center + diffusion * (extended[..., 2:, :] + extended[..., :-2, :] + column_pair(center) - 4.0 * center)


def refine(coarse, extended):
    upper = near_weight * coarse + far_weight * extended[..., :-2, :]
    lower = near_weight * coarse + far_weight * extended[..., 2:, :]
    rows_fine = jnp.stack([upper, lower], axis=-2)
    rows_fine = rows_fine.reshape(coarse.shape[:-2] + (2 * coarse.shape[-2], coarse.shape[-1]))
    padded = jnp.pad(rows_fine, [(0, 0)] * (rows_fine.ndim - 1) + [(1, 1)])
    left = near_weight * rows_fine + far_weight * padded[..., :-2]
    right = near_weight * rows_fine + far_weight * padded[..., 2:]
    both = jnp.stack([left, right], axis=-1)
    return both.reshape(rows_fine.shape[:-1] + (2 * rows_fine.shape[-1],))


def coarsen(fine_field, extended):
    half_rows = fine_field.shape[-2] // 2
    rows_coarse = near_weight * (fine_field[..., 0::2, :] + fine_field[..., 1::2, :])
    rows_coarse = rows_coarse + far_weight * (extended[..., 0:2 * half_rows:2, :] + extended[..., 3::2, :])
    width = rows_coarse.shape[-1]
    padded = jnp.pad(rows_coarse, [(0, 0)] * (rows_coarse.ndim - 1) + [(1, 1)])
    result = near_weight * (rows_coarse[..., 0::2] + rows_coarse[..., 1::2])
    return result + far_weight * (padded[..., 0:width:2] + padded[..., 3::2])


def obs_masks(code):
    return [(code == which).astype(jnp.float32) for which in range(1, 5)]


def observe(fine_field, extended, masks, count, weights):
    padded = jnp.pad(fine_field, [(0, 0)] * (fine_field.ndim - 1) + [(1, 1)])
    diff = fine_field - masks[0] * extended[..., 2:, :] - masks[1] * extended[..., :-2, :]
    diff = diff - masks[2] * padded[..., 2:] - masks[3] * padded[..., :-2]
    return count.astype(jnp.float32) * weights[:, :, None, None] * diff


def adjoint_rows(forcing, masks, above, below):
    first = masks[0] * forcing
    second = masks[1] * forcing
    from_above = jnp.concatenate([above, first[..., :-1, :]], axis=-2)
    from_below = jnp.concatenate([second[..., 1:, :], below], axis=-2)
    pad_spec = [(0, 0)] * (forcing.ndim - 1) + [(1, 1)]
    from_left = jnp.pad(masks[2] * forcing, pad_spec)[..., :-2]
    from_right = jnp.pad(masks[3] * forcing, pad_spec)[..., 2:]
    return forcing - from_above - from_below - from_left - from_right


def smooth_twice(field):
    return smooth_rows(row_margin(smooth_rows(row_margin(field))))


def reference(ensemble, control, vertical, inverse_var, obs_code, obs_count):
    factor = MEMBERS ** -0.5
    vertical_wide = vertical.astype(jnp.float32)

    def accumulate(total, pair):
        member_pert, member_control = pair
        mixed = jnp.einsum("lm,mxy->lxy", vertical_wide, member_control.astype(jnp.float32), precision=lax.Precision.HIGHEST)
        local = smooth_twice(mixed)
        return total + factor * member_pert.astype(jnp.float32) * local[None], None

    increment, _ = lax.scan(accumulate, jnp.zeros((VARS, LEV, NX, CY), jnp.float32), (ensemble, control))
    fine_field = refine(increment, row_margin(increment))
    masks = obs_masks(obs_code)
    forcing = observe(fine_field, row_margin(fine_field), masks, obs_count, inverse_var)
    edge = jnp.zeros(forcing.shape[:-2] + (1, forcing.shape[-1]), jnp.float32)
    adjoint_fine = adjoint_rows(forcing, masks, edge, edge)
    adjoint = coarsen(adjoint_fine, row_margin(adjoint_fine))

    def gradient(pair):
        member_pert, member_control = pair
        projected = factor * jnp.sum(member_pert.astype(jnp.float32) * adjoint, axis=0)
        rounded = smooth_twice(projected).astype(jnp.bfloat16)
        back = jnp.einsum("ml,mxy->lxy", vertical_wide, rounded.astype(jnp.float32), precision=lax.Precision.HIGHEST)
        return member_control.astype(jnp.float32) + back

    return lax.map(gradient, (ensemble, control))
```

```python
import functools
import jax
import jax.numpy as jnp
from jax import lax
from jax.experimental import pallas as pl
from jax.experimental.pallas import tpu as pltpu
from jax.sharding import PartitionSpec as P

diffusion = 0.2
near_weight = 0.75
far_weight = 0.25
f32 = jnp.float32
MESH = pl.DeviceIdType.MESH


def columns(x, by):
    width = x.shape[-1]
    lane = lax.broadcasted_iota(jnp.int32, x.shape, x.ndim - 1)
    moved = pltpu.roll(x, by % width, x.ndim - 1)
    edge = 0 if by == 1 else width - 1
    return jnp.where(lane == edge, 0.0, moved)


def smooth(prev, center, after):
    sides = columns(center, 1) + columns(center, -1)
    return center + diffusion * (after + prev + sides - 4.0 * center)


def smooth_twice(rows, low, high):
    first = [smooth(rows[i - 1], rows[i], rows[i + 1]) for i in range(1, len(rows) - 1)]
    first[0] = first[0] * low
    first[-1] = first[-1] * high
    return [smooth(first[i - 1], first[i], first[i + 1]) for i in range(1, len(first) - 1)]


def kernel(cfg, ens_hbm, ctl_ref, vert_ref, ivar_ref, code_ref, count_ref, out_ref,
           ens_ref, ensf, ctlf, ext, part, r1, half, r2, share, adj, proj, obs, rnd,
           ens_sem, a_s, a_r, b1_s, b1_r, b2_s, b2_r, c_s, c_r, d_s, d_r, p_s, p_r, e_s, e_r, o_s, o_r):
    KC, Q, M, G, R, KM, V, L, n, W, group = cfg
    NB = L // n
    HB = 2 * Q
    factor = (KM * M) ** (-0.5)
    mem = lax.axis_index("mem")
    grid = lax.axis_index("grid")
    core = lax.rem(mem, 2)
    chip = lax.div(mem, 2)
    partner = chip * 2 + (1 - core)
    has_prev = grid > 0
    has_next = grid < G - 1
    before = (mem, jnp.maximum(grid - 1, 0))
    behind = (mem, jnp.minimum(grid + 1, G - 1))
    low = jnp.where(has_prev, 1.0, 0.0).astype(f32)
    high = jnp.where(has_next, 1.0, 0.0).astype(f32)

    def peer(d):
        return (lax.rem(chip + d, Q) * 2 + core, grid)

    barrier = pltpu.get_barrier_semaphore()

    def greet(device):
        pl.semaphore_signal(barrier, inc=1, device_id=device, device_id_type=MESH)

    @pl.when(has_prev)
    def _():
        greet(before)

    @pl.when(has_next)
    def _():
        greet(behind)

    greet((partner, grid))
    for d in range(1, Q):
        greet(peer(d))

    ens_copy = pltpu.make_async_copy(ens_hbm, ens_ref, ens_sem)
    ens_copy.start()

    def up_copy(buf, lead, rows, s, r, at):
        return pltpu.make_async_remote_copy(
            src_ref=buf.at[lead + (pl.ds(rows, 2),)], dst_ref=buf.at[lead + (pl.ds(0, 2),)],
            send_sem=s.at[at, 0], recv_sem=r.at[at, 0], device_id=behind, device_id_type=MESH)

    def down_copy(buf, lead, rows, s, r, at):
        return pltpu.make_async_remote_copy(
            src_ref=buf.at[lead + (pl.ds(2, 2),)], dst_ref=buf.at[lead + (pl.ds(rows + 2, 2),)],
            send_sem=s.at[at, 1], recv_sem=r.at[at, 1], device_id=before, device_id_type=MESH)

    def halo_start(*args):
        @pl.when(has_next)
        def _():
            up_copy(*args).start()

        @pl.when(has_prev)
        def _():
            down_copy(*args).start()

    def halo_recv(*args):
        @pl.when(has_prev)
        def _():
            up_copy(*args).wait_recv()

        @pl.when(has_next)
        def _():
            down_copy(*args).wait_recv()

    def halo_sent(*args):
        @pl.when(has_next)
        def _():
            up_copy(*args).wait_send()

        @pl.when(has_prev)
        def _():
            down_copy(*args).wait_send()

    def a_args(j):
        return ext, (j,), R, a_s, a_r, j

    def c_args(j):
        return share, (j,), R, c_s, c_r, j

    def e_args(j):
        return proj, (j,), R, e_s, e_r, j

    o_args = (obs, (), 2 * R, o_s, o_r, 0)

    def core_copy(j):
        return pltpu.make_async_remote_copy(
            src_ref=part.at[j, 1 - core], dst_ref=r1.at[j], send_sem=b1_s.at[j], recv_sem=b1_r.at[j],
            device_id=(partner, grid), device_id_type=MESH)

    def chip_copy(j, d):
        return pltpu.make_async_remote_copy(
            src_ref=half.at[j, lax.rem(chip + d, Q)], dst_ref=r2.at[j, d],
            send_sem=b2_s.at[j, d], recv_sem=b2_r.at[j, d], device_id=peer(d), device_id_type=MESH)

    def gather_copy(j, d):
        return pltpu.make_async_remote_copy(
            src_ref=adj.at[j, core, chip], dst_ref=adj.at[j, core, chip],
            send_sem=d_s.at[j, d], recv_sem=d_r.at[j, d], device_id=peer(d), device_id_type=MESH)

    def pass_copy(j, d):
        source = lax.rem(chip + Q - d, Q)
        return pltpu.make_async_remote_copy(
            src_ref=adj.at[j, core, source], dst_ref=adj.at[j, core, source],
            send_sem=p_s.at[j, d], recv_sem=p_r.at[j, d], device_id=(partner, grid), device_id_type=MESH)

    ctlf[...] = ctl_ref[...].astype(f32)
    wide = jnp.concatenate(
        [ctlf[k, :, pl.ds(r, n, stride=R), :].reshape(L, W).astype(jnp.bfloat16)
         for k in range(KM) for r in range(R)], axis=1)
    mixed = jnp.dot(vert_ref[...], wide, preferred_element_type=f32)
    for k in range(KM):
        for r in range(R):
            at = (k * R + r) * W
            ext[:, 2 + r, k] = mixed[:, at:at + W].reshape(KC, HB, n, W)

    def pick():
        i = lax.broadcasted_iota(jnp.int32, (2 * W, 2 * W), 0)
        o = lax.broadcasted_iota(jnp.int32, (2 * W, 2 * W), 1)
        return jnp.where(i == 2 * lax.rem(o, W) + lax.div(o, W), 1.0, 0.0).astype(jnp.bfloat16)

    ints = jnp.concatenate([code_ref[...], count_ref[...]], axis=0).astype(f32).astype(jnp.bfloat16)
    apart = jnp.dot(ints, pick(), preferred_element_type=f32)
    for i in range(2 * R):
        for p in range(2):
            obs[2 + i, p:p + 1, :] = apart[i:i + 1, p * W:(p + 1) * W]
            obs[2 + i, 2 + p:3 + p, :] = apart[2 * R + i:2 * R + i + 1, p * W:(p + 1) * W]
        obs[2 + i, 4:8, :] = jnp.zeros((4, W), f32)

    @pl.when(jnp.logical_not(has_prev))
    def _():
        ext[:, 0:2] = jnp.zeros((KC, 2) + ext.shape[2:], f32)
        proj[:, 0:2] = jnp.zeros((KC, 2) + proj.shape[2:], f32)
        share[:, 0:2] = jnp.zeros((KC, 2) + share.shape[2:], f32)
        obs[0:2] = jnp.zeros((2,) + obs.shape[1:], f32)

    @pl.when(jnp.logical_not(has_next))
    def _():
        ext[:, R + 2:R + 4] = jnp.zeros((KC, 2) + ext.shape[2:], f32)
        proj[:, R + 2:R + 4] = jnp.zeros((KC, 2) + proj.shape[2:], f32)
        share[:, R + 2:R + 4] = jnp.zeros((KC, 2) + share.shape[2:], f32)
        obs[2 * R + 2:2 * R + 4] = jnp.zeros((2,) + obs.shape[1:], f32)

    pl.semaphore_wait(barrier, Q + has_prev.astype(jnp.int32) + has_next.astype(jnp.int32))

    for j in range(KC):
        halo_start(*a_args(j))
    halo_start(*o_args)

    ens_copy.wait()
    for k in range(KM):
        def widen(v, _):
            ensf[k, v] = ens_ref[k, v].astype(f32)
            return 0
        lax.fori_loop(0, V, widen, 0)

    halo_recv(*o_args)

    def member(k, v, b0, r):
        return ensf[k, v, pl.ds(b0, group), pl.ds(r, n, stride=R), :]

    for j in range(KC):
        halo_recv(*a_args(j))

        def weigh(g, _, j=j):
            b0 = g * group
            local = [smooth_twice([ext[j, i, k, pl.ds(b0, group)] for i in range(R + 4)], low, high)
                     for k in range(KM)]
            c, q0 = lax.div(b0, Q), lax.rem(b0, Q)
            for v in range(V):
                for r in range(R):
                    total = member(0, v, j * HB + b0, r) * local[0][r]
                    for k in range(1, KM):
                        total = total + member(k, v, j * HB + b0, r) * local[k][r]
                    part[j, c, pl.ds(q0, group), v, r] = factor * total
            return 0

        lax.fori_loop(0, HB // group, weigh, 0)
        core_copy(j).start()

    for j in range(KC):
        core_copy(j).wait_recv()

        def join(q, _, j=j):
            half[j, q] = part[j, core, q] + r1[j, q]
            return 0

        lax.fori_loop(0, Q, join, 0)
        for d in range(Q - 1, 0, -1):
            chip_copy(j, d).start()

    for j in range(KC):
        total = half[j, chip]
        for d in range(1, Q):
            chip_copy(j, d).wait_recv()
            total = total + r2[j, d]
        for r in range(R):
            share[j, 2 + r] = total[:, r]
        halo_start(*c_args(j))

    for j in range(KC):
        first_level = (j * HB + core * Q + chip) * n
        hot = (lax.broadcasted_iota(jnp.int32, (n, L), 1)
               == lax.broadcasted_iota(jnp.int32, (n, L), 0) + first_level)
        weights = jnp.stack(
            [jnp.broadcast_to(jnp.sum(jnp.where(hot, ivar_ref[v:v + 1, :], 0.0), axis=1, keepdims=True), (n, W))
             for v in range(V)], axis=0)
        halo_recv(*c_args(j))
        u = [share[j, i] for i in range(R + 4)]
        fine = []
        last = 2 * R + 3
        for i in range(last + 1):
            a = i // 2 + 1
            row = near_weight * u[a] + far_weight * (u[a - 1] if i % 2 == 0 else u[a + 1])
            if i < 2:
                row = row * low
            if i > last - 2:
                row = row * high
            fine.append((near_weight * row + far_weight * columns(row, 1),
                         near_weight * row + far_weight * columns(row, -1)))
        forced, ups, downs = [], [], []
        for i in range(last + 1):
            even_odd, up, down = [], [], []
            right_of = (fine[i][1], columns(fine[i][0], -1)) if 0 < i < last else None
            left_of = (columns(fine[i][1], 1), fine[i][0]) if 0 < i < last else None
            sides = []
            for p in range(2):
                code = obs[i, p:p + 1, :]
                scale = obs[i, 2 + p:3 + p, :] * weights
                m = [jnp.where(code == which, 1.0, 0.0) for which in range(1, 5)]
                diff = fine[i][p]
                if i < last:
                    diff = diff - m[0] * fine[i + 1][p]
                if i > 0:
                    diff = diff - m[1] * fine[i - 1][p]
                if right_of is not None:
                    diff = diff - m[2] * right_of[p] - m[3] * left_of[p]
                force = scale * diff
                even_odd.append(force)
                up.append(m[0] * force)
                down.append(m[1] * force)
                sides.append((m[2] * force, m[3] * force))
            ups.append(up)
            downs.append(down)
            if 0 < i < last:
                even = even_odd[0] - columns(sides[1][0], 1) - sides[1][1]
                odd = even_odd[1] - sides[0][0] - columns(sides[0][1], -1)
                forced.append((even, odd))
            else:
                forced.append(None)
        back = [None] * (last + 1)
        for i in range(1, last):
            pair = [forced[i][p] - ups[i - 1][p] - downs[i + 1][p] for p in range(2)]
            if i == 1:
                pair = [x * low for x in pair]
            if i == last - 1:
                pair = [x * high for x in pair]
            back[i] = pair
        for r in range(R):
            i = 2 * r + 2
            even, odd = [near_weight * (back[i][p] + back[i + 1][p]) + far_weight * (back[i - 1][p] + back[i + 2][p])
                         for p in range(2)]
            row = near_weight * (even + odd) + far_weight * (columns(odd, 1) + columns(even, -1))
            adj[j, core, chip, :, r] = row
        for d in range(Q - 1, 0, -1):
            gather_copy(j, d).start()
        pass_copy(j, 0).start()

    for j in range(KC):
        for d in range(1, Q):
            gather_copy(j, d).wait_recv()
            pass_copy(j, d).start()

    def arrived(j, d):
        source = lax.rem(chip + Q - d, Q)
        return pltpu.make_async_remote_copy(
            src_ref=adj.at[j, 1 - core, source], dst_ref=adj.at[j, 1 - core, source],
            send_sem=p_s.at[j, d], recv_sem=p_r.at[j, d], device_id=(partner, grid), device_id_type=MESH)

    for j in range(KC):
        for d in range(Q):
            arrived(j, d).wait_recv()

        def project(g, _, j=j):
            b0 = g * group
            c, q0 = lax.div(b0, Q), lax.rem(b0, Q)
            for r in range(R):
                fields = [adj[j, c, pl.ds(q0, group), v, r] for v in range(V)]
                for k in range(KM):
                    total = member(k, 0, j * HB + b0, r) * fields[0]
                    for v in range(1, V):
                        total = total + member(k, v, j * HB + b0, r) * fields[v]
                    proj[j, 2 + r, k, pl.ds(b0, group)] = factor * total
            return 0

        lax.fori_loop(0, HB // group, project, 0)
        halo_start(*e_args(j))

    for j in range(KC):
        halo_recv(*e_args(j))

        def settle(g, _, j=j):
            b0 = g * group
            for k in range(KM):
                rows = smooth_twice([proj[j, i, k, pl.ds(b0, group)] for i in range(R + 4)], low, high)
                for r in range(R):
                    rnd[k, r, pl.ds(j * HB + b0, group)] = rows[r]
            return 0

        lax.fori_loop(0, HB // group, settle, 0)

    wide = jnp.concatenate(
        [rnd[k, r].reshape(L, W).astype(jnp.bfloat16) for k in range(KM) for r in range(R)], axis=1)
    product = lax.dot_general(vert_ref[...], wide, (((0,), (0,)), ((), ())), preferred_element_type=f32)
    for k in range(KM):
        for r in range(R):
            at = (k * R + r) * W
            out_ref[k, :, pl.ds(r, n, stride=R), :] = (
                ctlf[k, :, pl.ds(r, n, stride=R), :] + product[:, at:at + W].reshape(NB, n, W))

    halo_sent(*o_args)
    for j in range(KC):
        halo_sent(*a_args(j))
        core_copy(j).wait_send()
        for d in range(1, Q):
            chip_copy(j, d).wait_send()
            gather_copy(j, d).wait_send()
        halo_sent(*c_args(j))
        for d in range(Q):
            pass_copy(j, d).wait_send()
        halo_sent(*e_args(j))


def per_device(ensemble, control, vertical, inverse_var, obs_code, obs_count):
    KM, V, L, R, W = ensemble.shape
    M = lax.axis_size("mem")
    G = lax.axis_size("grid")
    Q = M // 2
    levels = L // M
    KC = 2 if levels % 16 == 0 else 1
    n = levels // KC
    NB = L // n
    HB = 2 * Q
    group = 4 if Q % 4 == 0 else 1
    cfg = (KC, Q, M, G, R, KM, V, L, n, W, group)
    vmem = pl.BlockSpec(memory_space=pltpu.VMEM)
    dma = pltpu.SemaphoreType.DMA
    out = pl.pallas_call(
        functools.partial(kernel, cfg),
        out_shape=jax.ShapeDtypeStruct((KM, NB, n * R, W), f32),
        in_specs=[pl.BlockSpec(memory_space=pl.ANY)] + [vmem] * 5,
        out_specs=vmem,
        scratch_shapes=[
            pltpu.VMEM((KM, V, NB, n * R, W), jnp.bfloat16),
            pltpu.VMEM((KM, V, NB, n * R, W), f32),
            pltpu.VMEM((KM, NB, n * R, W), f32),
            pltpu.VMEM((KC, R + 4, KM, HB, n, W), f32),
            pltpu.VMEM((KC, 2, Q, V, R, n, W), f32),
            pltpu.VMEM((KC, Q, V, R, n, W), f32),
            pltpu.VMEM((KC, Q, V, R, n, W), f32),
            pltpu.VMEM((KC, Q, V, R, n, W), f32),
            pltpu.VMEM((KC, R + 4, V, n, W), f32),
            pltpu.VMEM((KC, 2, Q, V, R, n, W), f32),
            pltpu.VMEM((KC, R + 4, KM, HB, n, W), f32),
            pltpu.VMEM((2 * R + 4, 8, W), f32),
            pltpu.VMEM((KM, R, NB, n, W), f32),
            dma,
            dma((KC, 2)), dma((KC, 2)),
            dma((KC,)), dma((KC,)),
            dma((KC, Q)), dma((KC, Q)),
            dma((KC, 2)), dma((KC, 2)),
            dma((KC, Q)), dma((KC, Q)),
            dma((KC, Q)), dma((KC, Q)),
            dma((KC, 2)), dma((KC, 2)),
            dma((1, 2)), dma((1, 2)),
        ],
        compiler_params=pltpu.CompilerParams(collective_id=0, has_side_effects=True),
    )(
        ensemble.reshape(KM, V, NB, n * R, W),
        control.reshape(KM, NB, n * R, W),
        vertical,
        inverse_var,
        obs_code,
        obs_count,
    )
    return out.reshape(KM, L, R, W)


def solution(mesh):
    return jax.shard_map(
        per_device,
        mesh=mesh,
        in_specs=(
            P("mem", None, None, "grid", None),
            P("mem", None, "grid", None),
            P(),
            P(),
            P("grid", None),
            P("grid", None),
        ),
        out_specs=P("mem", None, "grid", None),
        check_vma=False,
    )
```

```python
import functools
import jax
import jax.numpy as jnp
from jax import lax
from jax.experimental import pallas as pl
from jax.experimental.pallas import tpu as pltpu
from jax.sharding import PartitionSpec as P

diffusion = 0.2
near_weight = 0.75
far_weight = 0.25
f32 = jnp.float32
MESH = pl.DeviceIdType.MESH


def columns(x, by):
    width = x.shape[-1]
    lane = lax.broadcasted_iota(jnp.int32, x.shape, x.ndim - 1)
    moved = pltpu.roll(x, by % width, x.ndim - 1)
    edge = 0 if by == 1 else width - 1
    return jnp.where(lane == edge, 0.0, moved)


def smooth(prev, center, after):
    sides = columns(center, 1) + columns(center, -1)
    return center + diffusion * (after + prev + sides - 4.0 * center)


def smooth_twice(rows, low, high):
    first = [smooth(rows[i - 1], rows[i], rows[i + 1]) for i in range(1, len(rows) - 1)]
    first[0] = first[0] * low
    first[-1] = first[-1] * high
    return [smooth(first[i - 1], first[i], first[i + 1]) for i in range(1, len(first) - 1)]


LAG = (0, 15, 45, 70, 95, 105, 150)


def order_of(chunks, count):
    delay = 28
    at = [(LAG[i] + delay * j, j, i) for j in range(chunks) for i in range(count)]
    return [(i, j) for _, j, i in sorted(at)]


def kernel(cfg, ens_hbm, ctl_ref, vert_ref, ivar_ref, code_ref, count_ref, out_ref,
           ens_ref, ensf, ctlf, ext, part, r1, half, r2, share, adj, proj, obs, rnd,
           ens_sem, a_s, a_r, b1_s, b1_r, b2_s, b2_r, c_s, c_r, d_s, d_r, p_s, p_r, e_s, e_r, o_s, o_r):
    KC, Q, M, G, R, KM, V, L, n, W, group = cfg
    NB = L // n
    HB = 2 * Q
    factor = (KM * M) ** (-0.5)
    mem = lax.axis_index("mem")
    grid = lax.axis_index("grid")
    core = lax.rem(mem, 2)
    chip = lax.div(mem, 2)
    partner = chip * 2 + (1 - core)
    has_prev = grid > 0
    has_next = grid < G - 1
    before = (mem, jnp.maximum(grid - 1, 0))
    behind = (mem, jnp.minimum(grid + 1, G - 1))
    low = jnp.where(has_prev, 1.0, 0.0).astype(f32)
    high = jnp.where(has_next, 1.0, 0.0).astype(f32)

    def peer(d):
        return (lax.rem(chip + d, Q) * 2 + core, grid)

    barrier = pltpu.get_barrier_semaphore()

    def greet(device):
        pl.semaphore_signal(barrier, inc=1, device_id=device, device_id_type=MESH)

    @pl.when(has_prev)
    def _():
        greet(before)

    @pl.when(has_next)
    def _():
        greet(behind)

    greet((partner, grid))
    for d in range(1, Q):
        greet(peer(d))

    ens_copy = pltpu.make_async_copy(ens_hbm, ens_ref, ens_sem)
    ens_copy.start()

    def up_copy(buf, lead, rows, s, r, at):
        return pltpu.make_async_remote_copy(
            src_ref=buf.at[lead + (pl.ds(rows, 2),)], dst_ref=buf.at[lead + (pl.ds(0, 2),)],
            send_sem=s.at[at, 0], recv_sem=r.at[at, 0], device_id=behind, device_id_type=MESH)

    def down_copy(buf, lead, rows, s, r, at):
        return pltpu.make_async_remote_copy(
            src_ref=buf.at[lead + (pl.ds(2, 2),)], dst_ref=buf.at[lead + (pl.ds(rows + 2, 2),)],
            send_sem=s.at[at, 1], recv_sem=r.at[at, 1], device_id=before, device_id_type=MESH)

    def halo_start(*args):
        @pl.when(has_next)
        def _():
            up_copy(*args).start()

        @pl.when(has_prev)
        def _():
            down_copy(*args).start()

    def halo_recv(*args):
        @pl.when(has_prev)
        def _():
            up_copy(*args).wait_recv()

        @pl.when(has_next)
        def _():
            down_copy(*args).wait_recv()

    def halo_sent(*args):
        @pl.when(has_next)
        def _():
            up_copy(*args).wait_send()

        @pl.when(has_prev)
        def _():
            down_copy(*args).wait_send()

    def a_args(j):
        return ext, (j,), R, a_s, a_r, j

    def c_args(j):
        return share, (j,), R, c_s, c_r, j

    def e_args(j):
        return proj, (j,), R, e_s, e_r, j

    o_args = (obs, (), 2 * R, o_s, o_r, 0)

    def core_copy(j):
        return pltpu.make_async_remote_copy(
            src_ref=part.at[j, 1 - core], dst_ref=r1.at[j], send_sem=b1_s.at[j], recv_sem=b1_r.at[j],
            device_id=(partner, grid), device_id_type=MESH)

    def chip_copy(j, d):
        return pltpu.make_async_remote_copy(
            src_ref=half.at[j, lax.rem(chip + d, Q)], dst_ref=r2.at[j, d],
            send_sem=b2_s.at[j, d], recv_sem=b2_r.at[j, d], device_id=peer(d), device_id_type=MESH)

    def gather_copy(j, d):
        return pltpu.make_async_remote_copy(
            src_ref=adj.at[j, core, chip], dst_ref=adj.at[j, core, chip],
            send_sem=d_s.at[j, d], recv_sem=d_r.at[j, d], device_id=peer(d), device_id_type=MESH)

    def pass_copy(j, d):
        source = lax.rem(chip + Q - d, Q)
        return pltpu.make_async_remote_copy(
            src_ref=adj.at[j, core, source], dst_ref=adj.at[j, core, source],
            send_sem=p_s.at[j, d], recv_sem=p_r.at[j, d], device_id=(partner, grid), device_id_type=MESH)

    ctlf[...] = ctl_ref[...].astype(f32)
    wide = jnp.concatenate(
        [ctlf[k, :, pl.ds(r, n, stride=R), :].reshape(L, W).astype(jnp.bfloat16)
         for k in range(KM) for r in range(R)], axis=1)
    mixed = jnp.dot(vert_ref[...], wide, preferred_element_type=f32)
    for k in range(KM):
        for r in range(R):
            at = (k * R + r) * W
            ext[:, 2 + r, k] = mixed[:, at:at + W].reshape(KC, HB, n, W)

    def pick():
        i = lax.broadcasted_iota(jnp.int32, (2 * W, 2 * W), 0)
        o = lax.broadcasted_iota(jnp.int32, (2 * W, 2 * W), 1)
        return jnp.where(i == 2 * lax.rem(o, W) + lax.div(o, W), 1.0, 0.0).astype(jnp.bfloat16)

    ints = jnp.concatenate([code_ref[...], count_ref[...]], axis=0).astype(f32).astype(jnp.bfloat16)
    apart = jnp.dot(ints, pick(), preferred_element_type=f32)
    for i in range(2 * R):
        for p in range(2):
            obs[2 + i, p:p + 1, :] = apart[i:i + 1, p * W:(p + 1) * W]
            obs[2 + i, 2 + p:3 + p, :] = apart[2 * R + i:2 * R + i + 1, p * W:(p + 1) * W]
        obs[2 + i, 4:8, :] = jnp.zeros((4, W), f32)

    @pl.when(jnp.logical_not(has_prev))
    def _():
        ext[:, 0:2] = jnp.zeros((KC, 2) + ext.shape[2:], f32)
        proj[:, 0:2] = jnp.zeros((KC, 2) + proj.shape[2:], f32)
        share[:, 0:2] = jnp.zeros((KC, 2) + share.shape[2:], f32)
        obs[0:2] = jnp.zeros((2,) + obs.shape[1:], f32)

    @pl.when(jnp.logical_not(has_next))
    def _():
        ext[:, R + 2:R + 4] = jnp.zeros((KC, 2) + ext.shape[2:], f32)
        proj[:, R + 2:R + 4] = jnp.zeros((KC, 2) + proj.shape[2:], f32)
        share[:, R + 2:R + 4] = jnp.zeros((KC, 2) + share.shape[2:], f32)
        obs[2 * R + 2:2 * R + 4] = jnp.zeros((2,) + obs.shape[1:], f32)

    pl.semaphore_wait(barrier, Q + has_prev.astype(jnp.int32) + has_next.astype(jnp.int32))

    for j in range(KC):
        halo_start(*a_args(j))
    halo_start(*o_args)

    ens_copy.wait()
    for k in range(KM):
        def widen(v, _):
            ensf[k, v] = ens_ref[k, v].astype(f32)
            return 0
        lax.fori_loop(0, V, widen, 0)

    halo_recv(*o_args)

    def member(k, v, b0, r):
        return ensf[k, v, pl.ds(b0, group), pl.ds(r, n, stride=R), :]

    def stage_weigh(j):
        halo_recv(*a_args(j))

        def weigh(g, _):
            b0 = g * group
            local = [smooth_twice([ext[j, i, k, pl.ds(b0, group)] for i in range(R + 4)], low, high)
                     for k in range(KM)]
            c, q0 = lax.div(b0, Q), lax.rem(b0, Q)
            for v in range(V):
                for r in range(R):
                    total = member(0, v, j * HB + b0, r) * local[0][r]
                    for k in range(1, KM):
                        total = total + member(k, v, j * HB + b0, r) * local[k][r]
                    part[j, c, pl.ds(q0, group), v, r] = factor * total
            return 0

        lax.fori_loop(0, HB // group, weigh, 0)
        core_copy(j).start()

    def stage_join(j):
        core_copy(j).wait_recv()

        def join(q, _):
            half[j, q] = part[j, core, q] + r1[j, q]
            return 0

        lax.fori_loop(0, Q, join, 0)
        for d in range(Q - 1, 0, -1):
            chip_copy(j, d).start()

    def stage_reduce(j):
        total = half[j, chip]
        for d in range(1, Q):
            chip_copy(j, d).wait_recv()
            total = total + r2[j, d]
        for r in range(R):
            share[j, 2 + r] = total[:, r]
        halo_start(*c_args(j))

    def stage_observe(j):
        first_level = (j * HB + core * Q + chip) * n
        hot = (lax.broadcasted_iota(jnp.int32, (n, L), 1)
               == lax.broadcasted_iota(jnp.int32, (n, L), 0) + first_level)
        weights = jnp.stack(
            [jnp.broadcast_to(jnp.sum(jnp.where(hot, ivar_ref[v:v + 1, :], 0.0), axis=1, keepdims=True), (n, W))
             for v in range(V)], axis=0)
        halo_recv(*c_args(j))
        u = [share[j, i] for i in range(R + 4)]
        fine = []
        last = 2 * R + 3
        for i in range(last + 1):
            a = i // 2 + 1
            row = near_weight * u[a] + far_weight * (u[a - 1] if i % 2 == 0 else u[a + 1])
            if i < 2:
                row = row * low
            if i > last - 2:
                row = row * high
            fine.append((near_weight * row + far_weight * columns(row, 1),
                         near_weight * row + far_weight * columns(row, -1)))
        forced, ups, downs = [], [], []
        for i in range(last + 1):
            even_odd, up, down = [], [], []
            right_of = (fine[i][1], columns(fine[i][0], -1)) if 0 < i < last else None
            left_of = (columns(fine[i][1], 1), fine[i][0]) if 0 < i < last else None
            sides = []
            for p in range(2):
                code = obs[i, p:p + 1, :]
                scale = obs[i, 2 + p:3 + p, :] * weights
                m = [jnp.where(code == which, 1.0, 0.0) for which in range(1, 5)]
                diff = fine[i][p]
                if i < last:
                    diff = diff - m[0] * fine[i + 1][p]
                if i > 0:
                    diff = diff - m[1] * fine[i - 1][p]
                if right_of is not None:
                    diff = diff - m[2] * right_of[p] - m[3] * left_of[p]
                force = scale * diff
                even_odd.append(force)
                up.append(m[0] * force)
                down.append(m[1] * force)
                sides.append((m[2] * force, m[3] * force))
            ups.append(up)
            downs.append(down)
            if 0 < i < last:
                even = even_odd[0] - columns(sides[1][0], 1) - sides[1][1]
                odd = even_odd[1] - sides[0][0] - columns(sides[0][1], -1)
                forced.append((even, odd))
            else:
                forced.append(None)
        back = [None] * (last + 1)
        for i in range(1, last):
            pair = [forced[i][p] - ups[i - 1][p] - downs[i + 1][p] for p in range(2)]
            if i == 1:
                pair = [x * low for x in pair]
            if i == last - 1:
                pair = [x * high for x in pair]
            back[i] = pair
        for r in range(R):
            i = 2 * r + 2
            even, odd = [near_weight * (back[i][p] + back[i + 1][p]) + far_weight * (back[i - 1][p] + back[i + 2][p])
                         for p in range(2)]
            row = near_weight * (even + odd) + far_weight * (columns(odd, 1) + columns(even, -1))
            adj[j, core, chip, :, r] = row
        for d in range(Q - 1, 0, -1):
            gather_copy(j, d).start()
        pass_copy(j, 0).start()

    def stage_forward(j):
        for d in range(1, Q):
            gather_copy(j, d).wait_recv()
            pass_copy(j, d).start()

    def arrived(j, d):
        source = lax.rem(chip + Q - d, Q)
        return pltpu.make_async_remote_copy(
            src_ref=adj.at[j, 1 - core, source], dst_ref=adj.at[j, 1 - core, source],
            send_sem=p_s.at[j, d], recv_sem=p_r.at[j, d], device_id=(partner, grid), device_id_type=MESH)

    def stage_project(j):
        for d in range(Q):
            arrived(j, d).wait_recv()

        def project(g, _):
            b0 = g * group
            c, q0 = lax.div(b0, Q), lax.rem(b0, Q)
            for r in range(R):
                fields = [adj[j, c, pl.ds(q0, group), v, r] for v in range(V)]
                for k in range(KM):
                    total = member(k, 0, j * HB + b0, r) * fields[0]
                    for v in range(1, V):
                        total = total + member(k, v, j * HB + b0, r) * fields[v]
                    proj[j, 2 + r, k, pl.ds(b0, group)] = factor * total
            return 0

        lax.fori_loop(0, HB // group, project, 0)
        halo_start(*e_args(j))

    def stage_settle(j):
        halo_recv(*e_args(j))

        def settle(g, _):
            b0 = g * group
            for k in range(KM):
                rows = smooth_twice([proj[j, i, k, pl.ds(b0, group)] for i in range(R + 4)], low, high)
                for r in range(R):
                    rnd[k, r, pl.ds(j * HB + b0, group)] = rows[r]
            return 0

        lax.fori_loop(0, HB // group, settle, 0)

    stages = (stage_weigh, stage_join, stage_reduce, stage_observe, stage_forward, stage_project, stage_settle)
    for index, j in order_of(KC, len(stages)):
        stages[index](j)

    wide = jnp.concatenate(
        [rnd[k, r].reshape(L, W).astype(jnp.bfloat16) for k in range(KM) for r in range(R)], axis=1)
    product = lax.dot_general(vert_ref[...], wide, (((0,), (0,)), ((), ())), preferred_element_type=f32)
    for k in range(KM):
        for r in range(R):
            at = (k * R + r) * W
            out_ref[k, :, pl.ds(r, n, stride=R), :] = product[:, at:at + W].reshape(NB, n, W)

    halo_sent(*o_args)
    for j in range(KC):
        halo_sent(*a_args(j))
        core_copy(j).wait_send()
        for d in range(1, Q):
            chip_copy(j, d).wait_send()
            gather_copy(j, d).wait_send()
        halo_sent(*c_args(j))
        for d in range(Q):
            pass_copy(j, d).wait_send()
        halo_sent(*e_args(j))


def per_device(ensemble, control, vertical, inverse_var, obs_code, obs_count):
    KM, V, L, R, W = ensemble.shape
    M = lax.axis_size("mem")
    G = lax.axis_size("grid")
    Q = M // 2
    levels = L // M
    KC = 2 if levels % 16 == 0 else 1
    n = levels // KC
    NB = L // n
    HB = 2 * Q
    group = 4 if Q % 4 == 0 else 1
    cfg = (KC, Q, M, G, R, KM, V, L, n, W, group)
    vmem = pl.BlockSpec(memory_space=pltpu.VMEM)
    dma = pltpu.SemaphoreType.DMA
    member_control = control.reshape(KM, NB, n * R, W)
    back = pl.pallas_call(
        functools.partial(kernel, cfg),
        out_shape=jax.ShapeDtypeStruct((KM, NB, n * R, W), f32),
        in_specs=[pl.BlockSpec(memory_space=pl.ANY)] + [vmem] * 5,
        out_specs=vmem,
        scratch_shapes=[
            pltpu.VMEM((KM, V, NB, n * R, W), jnp.bfloat16),
            pltpu.VMEM((KM, V, NB, n * R, W), f32),
            pltpu.VMEM((KM, NB, n * R, W), f32),
            pltpu.VMEM((KC, R + 4, KM, HB, n, W), f32),
            pltpu.VMEM((KC, 2, Q, V, R, n, W), f32),
            pltpu.VMEM((KC, Q, V, R, n, W), f32),
            pltpu.VMEM((KC, Q, V, R, n, W), f32),
            pltpu.VMEM((KC, Q, V, R, n, W), f32),
            pltpu.VMEM((KC, R + 4, V, n, W), f32),
            pltpu.VMEM((KC, 2, Q, V, R, n, W), f32),
            pltpu.VMEM((KC, R + 4, KM, HB, n, W), f32),
            pltpu.VMEM((2 * R + 4, 8, W), f32),
            pltpu.VMEM((KM, R, NB, n, W), f32),
            dma,
            dma((KC, 2)), dma((KC, 2)),
            dma((KC,)), dma((KC,)),
            dma((KC, Q)), dma((KC, Q)),
            dma((KC, 2)), dma((KC, 2)),
            dma((KC, Q)), dma((KC, Q)),
            dma((KC, Q)), dma((KC, Q)),
            dma((KC, 2)), dma((KC, 2)),
            dma((1, 2)), dma((1, 2)),
        ],
        compiler_params=pltpu.CompilerParams(collective_id=0, has_side_effects=True),
    )(
        ensemble.reshape(KM, V, NB, n * R, W),
        member_control,
        vertical,
        inverse_var,
        obs_code,
        obs_count,
    )
    return (member_control.astype(f32) + back).reshape(KM, L, R, W)


def solution(mesh):
    return jax.shard_map(
        per_device,
        mesh=mesh,
        in_specs=(
            P("mem", None, None, "grid", None),
            P("mem", None, "grid", None),
            P(),
            P(),
            P("grid", None),
            P("grid", None),
        ),
        out_specs=P("mem", None, "grid", None),
        check_vma=False,
    )
```

```python
import functools
import jax
import jax.numpy as jnp
from jax import lax
from jax.experimental import pallas as pl
from jax.experimental.pallas import tpu as pltpu
from jax.sharding import PartitionSpec as P

diffusion = 0.2
near_weight = 0.75
far_weight = 0.25
f32 = jnp.float32
MESH = pl.DeviceIdType.MESH


def columns(x, by):
    width = x.shape[-1]
    lane = lax.broadcasted_iota(jnp.int32, x.shape, x.ndim - 1)
    moved = pltpu.roll(x, by % width, x.ndim - 1)
    edge = 0 if by == 1 else width - 1
    return jnp.where(lane == edge, 0.0, moved)


def smooth(prev, center, after):
    sides = columns(center, 1) + columns(center, -1)
    return center + diffusion * (after + prev + sides - 4.0 * center)


def smooth_twice(rows, low, high):
    first = [smooth(rows[i - 1], rows[i], rows[i + 1]) for i in range(1, len(rows) - 1)]
    first[0] = first[0] * low
    first[-1] = first[-1] * high
    return [smooth(first[i - 1], first[i], first[i + 1]) for i in range(1, len(first) - 1)]


LAG = (0, 20, 60, 90, 130, 140, 190)


def order_of(chunks, count):
    delay = 35
    at = [(LAG[i] + delay * j, j, i) for j in range(chunks) for i in range(count)]
    return [(i, j) for _, j, i in sorted(at)]


def kernel(cfg, ens_hbm, ctl_hbm, vert_hbm, ivar_hbm, code_hbm, count_hbm, out_ref,
           ens_ref, ctl_ref, vert_ref, ivar_ref, code_ref, count_ref, ensf, ctlf, ext, part, r1, half, r2, share, adj, proj, obs, rnd,
           in_sem, a_s, a_r, b1_s, b1_r, b2_s, b2_r, c_s, c_r, d_s, d_r, p_s, p_r, e_s, e_r, o_s, o_r):
    KC, Q, M, G, R, KM, V, L, n, W, group = cfg
    NB = L // n
    HB = 2 * Q
    factor = (KM * M) ** (-0.5)
    mem = lax.axis_index("mem")
    grid = lax.axis_index("grid")
    core = lax.rem(mem, 2)
    chip = lax.div(mem, 2)
    partner = chip * 2 + (1 - core)
    has_prev = grid > 0
    has_next = grid < G - 1
    before = (mem, jnp.maximum(grid - 1, 0))
    behind = (mem, jnp.minimum(grid + 1, G - 1))
    low = jnp.where(has_prev, 1.0, 0.0).astype(f32)
    high = jnp.where(has_next, 1.0, 0.0).astype(f32)

    def peer(d):
        return (lax.rem(chip + d, Q) * 2 + core, grid)

    barrier = pltpu.get_barrier_semaphore()

    def greet(device):
        pl.semaphore_signal(barrier, inc=1, device_id=device, device_id_type=MESH)

    @pl.when(has_prev)
    def _():
        greet(before)

    @pl.when(has_next)
    def _():
        greet(behind)

    greet((partner, grid))
    for d in range(1, Q):
        greet(peer(d))

    loads = [pltpu.make_async_copy(source, target, in_sem.at[i]) for i, (source, target) in enumerate((
        (ctl_hbm, ctl_ref), (vert_hbm, vert_ref), (code_hbm, code_ref), (count_hbm, count_ref),
        (ivar_hbm, ivar_ref), (ens_hbm, ens_ref)))]
    for load in loads:
        load.start()

    def up_copy(buf, lead, rows, s, r, at):
        return pltpu.make_async_remote_copy(
            src_ref=buf.at[lead + (pl.ds(rows, 2),)], dst_ref=buf.at[lead + (pl.ds(0, 2),)],
            send_sem=s.at[at, 0], recv_sem=r.at[at, 0], device_id=behind, device_id_type=MESH)

    def down_copy(buf, lead, rows, s, r, at):
        return pltpu.make_async_remote_copy(
            src_ref=buf.at[lead + (pl.ds(2, 2),)], dst_ref=buf.at[lead + (pl.ds(rows + 2, 2),)],
            send_sem=s.at[at, 1], recv_sem=r.at[at, 1], device_id=before, device_id_type=MESH)

    def halo_start(*args):
        @pl.when(has_next)
        def _():
            up_copy(*args).start()

        @pl.when(has_prev)
        def _():
            down_copy(*args).start()

    def halo_recv(*args):
        @pl.when(has_prev)
        def _():
            up_copy(*args).wait_recv()

        @pl.when(has_next)
        def _():
            down_copy(*args).wait_recv()

    def halo_sent(*args):
        @pl.when(has_next)
        def _():
            up_copy(*args).wait_send()

        @pl.when(has_prev)
        def _():
            down_copy(*args).wait_send()

    def a_args(j):
        return ext, (j,), R, a_s, a_r, j

    def c_args(j):
        return share, (j,), R, c_s, c_r, j

    def e_args(j):
        return proj, (j,), R, e_s, e_r, j

    o_args = (obs, (), 2 * R, o_s, o_r, 0)

    def core_copy(j):
        return pltpu.make_async_remote_copy(
            src_ref=part.at[j, 1 - core], dst_ref=r1.at[j], send_sem=b1_s.at[j], recv_sem=b1_r.at[j],
            device_id=(partner, grid), device_id_type=MESH)

    def chip_copy(j, d):
        return pltpu.make_async_remote_copy(
            src_ref=half.at[j, lax.rem(chip + d, Q)], dst_ref=r2.at[j, d],
            send_sem=b2_s.at[j, d], recv_sem=b2_r.at[j, d], device_id=peer(d), device_id_type=MESH)

    def gather_copy(j, d):
        return pltpu.make_async_remote_copy(
            src_ref=adj.at[j, core, chip], dst_ref=adj.at[j, core, chip],
            send_sem=d_s.at[j, d], recv_sem=d_r.at[j, d], device_id=peer(d), device_id_type=MESH)

    def pass_copy(j, d):
        source = lax.rem(chip + Q - d, Q)
        return pltpu.make_async_remote_copy(
            src_ref=adj.at[j, core, source], dst_ref=adj.at[j, core, source],
            send_sem=p_s.at[j, d], recv_sem=p_r.at[j, d], device_id=(partner, grid), device_id_type=MESH)

    loads[0].wait()
    loads[1].wait()
    ctlf[...] = ctl_ref[...].astype(f32)
    wide = jnp.concatenate(
        [ctlf[k, :, pl.ds(r, n, stride=R), :].reshape(L, W).astype(jnp.bfloat16)
         for k in range(KM) for r in range(R)], axis=1)
    mixed = jnp.dot(vert_ref[...], wide, preferred_element_type=f32)
    for k in range(KM):
        for r in range(R):
            at = (k * R + r) * W
            ext[:, 2 + r, k] = mixed[:, at:at + W].reshape(KC, HB, n, W)

    def pick():
        i = lax.broadcasted_iota(jnp.int32, (2 * W, 2 * W), 0)
        o = lax.broadcasted_iota(jnp.int32, (2 * W, 2 * W), 1)
        return jnp.where(i == 2 * lax.rem(o, W) + lax.div(o, W), 1.0, 0.0).astype(jnp.bfloat16)

    loads[2].wait()
    loads[3].wait()
    ints = jnp.concatenate([code_ref[...], count_ref[...]], axis=0).astype(f32).astype(jnp.bfloat16)
    apart = jnp.dot(ints, pick(), preferred_element_type=f32)
    for i in range(2 * R):
        for p in range(2):
            obs[2 + i, p:p + 1, :] = apart[i:i + 1, p * W:(p + 1) * W]
            obs[2 + i, 2 + p:3 + p, :] = apart[2 * R + i:2 * R + i + 1, p * W:(p + 1) * W]
        obs[2 + i, 4:8, :] = jnp.zeros((4, W), f32)

    @pl.when(jnp.logical_not(has_prev))
    def _():
        ext[:, 0:2] = jnp.zeros((KC, 2) + ext.shape[2:], f32)
        proj[:, 0:2] = jnp.zeros((KC, 2) + proj.shape[2:], f32)
        share[:, 0:2] = jnp.zeros((KC, 2) + share.shape[2:], f32)
        obs[0:2] = jnp.zeros((2,) + obs.shape[1:], f32)

    @pl.when(jnp.logical_not(has_next))
    def _():
        ext[:, R + 2:R + 4] = jnp.zeros((KC, 2) + ext.shape[2:], f32)
        proj[:, R + 2:R + 4] = jnp.zeros((KC, 2) + proj.shape[2:], f32)
        share[:, R + 2:R + 4] = jnp.zeros((KC, 2) + share.shape[2:], f32)
        obs[2 * R + 2:2 * R + 4] = jnp.zeros((2,) + obs.shape[1:], f32)

    pl.semaphore_wait(barrier, Q + has_prev.astype(jnp.int32) + has_next.astype(jnp.int32))

    for j in range(KC):
        halo_start(*a_args(j))
    halo_start(*o_args)

    loads[4].wait()
    loads[5].wait()
    for k in range(KM):
        def widen(v, _):
            ensf[k, v] = ens_ref[k, v].astype(f32)
            return 0
        lax.fori_loop(0, V, widen, 0)

    halo_recv(*o_args)

    def member(k, v, b0, r):
        return ensf[k, v, pl.ds(b0, group), pl.ds(r, n, stride=R), :]

    def stage_weigh(j):
        halo_recv(*a_args(j))

        def weigh(g, _):
            b0 = g * group
            local = [smooth_twice([ext[j, i, k, pl.ds(b0, group)] for i in range(R + 4)], low, high)
                     for k in range(KM)]
            c, q0 = lax.div(b0, Q), lax.rem(b0, Q)
            for v in range(V):
                for r in range(R):
                    total = member(0, v, j * HB + b0, r) * local[0][r]
                    for k in range(1, KM):
                        total = total + member(k, v, j * HB + b0, r) * local[k][r]
                    part[j, c, pl.ds(q0, group), v, r] = factor * total
            return 0

        lax.fori_loop(0, HB // group, weigh, 0)
        core_copy(j).start()

    def stage_join(j):
        core_copy(j).wait_recv()

        def join(q, _):
            half[j, q] = part[j, core, q] + r1[j, q]
            return 0

        lax.fori_loop(0, Q, join, 0)
        for d in range(Q - 1, 0, -1):
            chip_copy(j, d).start()

    def stage_reduce(j):
        total = half[j, chip]
        for d in range(1, Q):
            chip_copy(j, d).wait_recv()
            total = total + r2[j, d]
        for r in range(R):
            share[j, 2 + r] = total[:, r]
        halo_start(*c_args(j))

    def stage_observe(j):
        first_level = (j * HB + core * Q + chip) * n
        hot = (lax.broadcasted_iota(jnp.int32, (n, L), 1)
               == lax.broadcasted_iota(jnp.int32, (n, L), 0) + first_level)
        weights = jnp.stack(
            [jnp.broadcast_to(jnp.sum(jnp.where(hot, ivar_ref[v:v + 1, :], 0.0), axis=1, keepdims=True), (n, W))
             for v in range(V)], axis=0)
        halo_recv(*c_args(j))
        u = [share[j, i] for i in range(R + 4)]
        fine = []
        last = 2 * R + 3
        for i in range(last + 1):
            a = i // 2 + 1
            row = near_weight * u[a] + far_weight * (u[a - 1] if i % 2 == 0 else u[a + 1])
            if i < 2:
                row = row * low
            if i > last - 2:
                row = row * high
            fine.append((near_weight * row + far_weight * columns(row, 1),
                         near_weight * row + far_weight * columns(row, -1)))
        forced, ups, downs = [], [], []
        for i in range(last + 1):
            even_odd, up, down = [], [], []
            right_of = (fine[i][1], columns(fine[i][0], -1)) if 0 < i < last else None
            left_of = (columns(fine[i][1], 1), fine[i][0]) if 0 < i < last else None
            sides = []
            for p in range(2):
                code = obs[i, p:p + 1, :]
                scale = obs[i, 2 + p:3 + p, :] * weights
                m = [jnp.where(code == which, 1.0, 0.0) for which in range(1, 5)]
                diff = fine[i][p]
                if i < last:
                    diff = diff - m[0] * fine[i + 1][p]
                if i > 0:
                    diff = diff - m[1] * fine[i - 1][p]
                if right_of is not None:
                    diff = diff - m[2] * right_of[p] - m[3] * left_of[p]
                force = scale * diff
                even_odd.append(force)
                up.append(m[0] * force)
                down.append(m[1] * force)
                sides.append((m[2] * force, m[3] * force))
            ups.append(up)
            downs.append(down)
            if 0 < i < last:
                even = even_odd[0] - columns(sides[1][0], 1) - sides[1][1]
                odd = even_odd[1] - sides[0][0] - columns(sides[0][1], -1)
                forced.append((even, odd))
            else:
                forced.append(None)
        back = [None] * (last + 1)
        for i in range(1, last):
            pair = [forced[i][p] - ups[i - 1][p] - downs[i + 1][p] for p in range(2)]
            if i == 1:
                pair = [x * low for x in pair]
            if i == last - 1:
                pair = [x * high for x in pair]
            back[i] = pair
        for r in range(R):
            i = 2 * r + 2
            even, odd = [near_weight * (back[i][p] + back[i + 1][p]) + far_weight * (back[i - 1][p] + back[i + 2][p])
                         for p in range(2)]
            row = near_weight * (even + odd) + far_weight * (columns(odd, 1) + columns(even, -1))
            adj[j, core, chip, :, r] = row
        for d in range(Q - 1, 0, -1):
            gather_copy(j, d).start()
        pass_copy(j, 0).start()

    def stage_forward(j):
        for d in range(1, Q):
            gather_copy(j, d).wait_recv()
            pass_copy(j, d).start()

    def arrived(j, d):
        source = lax.rem(chip + Q - d, Q)
        return pltpu.make_async_remote_copy(
            src_ref=adj.at[j, 1 - core, source], dst_ref=adj.at[j, 1 - core, source],
            send_sem=p_s.at[j, d], recv_sem=p_r.at[j, d], device_id=(partner, grid), device_id_type=MESH)

    def stage_project(j):
        for d in range(Q):
            arrived(j, d).wait_recv()

        def project(g, _):
            b0 = g * group
            c, q0 = lax.div(b0, Q), lax.rem(b0, Q)
            for r in range(R):
                fields = [adj[j, c, pl.ds(q0, group), v, r] for v in range(V)]
                for k in range(KM):
                    total = member(k, 0, j * HB + b0, r) * fields[0]
                    for v in range(1, V):
                        total = total + member(k, v, j * HB + b0, r) * fields[v]
                    proj[j, 2 + r, k, pl.ds(b0, group)] = factor * total
            return 0

        lax.fori_loop(0, HB // group, project, 0)
        halo_start(*e_args(j))

    def stage_settle(j):
        halo_recv(*e_args(j))

        def settle(g, _):
            b0 = g * group
            for k in range(KM):
                rows = smooth_twice([proj[j, i, k, pl.ds(b0, group)] for i in range(R + 4)], low, high)
                for r in range(R):
                    rnd[k, r, pl.ds(j * HB + b0, group)] = rows[r]
            return 0

        lax.fori_loop(0, HB // group, settle, 0)

    stages = (stage_weigh, stage_join, stage_reduce, stage_observe, stage_forward, stage_project, stage_settle)
    for index, j in order_of(KC, len(stages)):
        stages[index](j)

    wide = jnp.concatenate(
        [rnd[k, r].reshape(L, W).astype(jnp.bfloat16) for k in range(KM) for r in range(R)], axis=1)
    product = lax.dot_general(vert_ref[...], wide, (((0,), (0,)), ((), ())), preferred_element_type=f32)
    for k in range(KM):
        for r in range(R):
            at = (k * R + r) * W
            out_ref[k, :, pl.ds(r, n, stride=R), :] = product[:, at:at + W].reshape(NB, n, W)

    halo_sent(*o_args)
    for j in range(KC):
        halo_sent(*a_args(j))
        core_copy(j).wait_send()
        for d in range(1, Q):
            chip_copy(j, d).wait_send()
            gather_copy(j, d).wait_send()
        halo_sent(*c_args(j))
        for d in range(Q):
            pass_copy(j, d).wait_send()
        halo_sent(*e_args(j))


def per_device(ensemble, control, vertical, inverse_var, obs_code, obs_count):
    KM, V, L, R, W = ensemble.shape
    M = lax.axis_size("mem")
    G = lax.axis_size("grid")
    Q = M // 2
    levels = L // M
    KC = 2 if levels % 16 == 0 else 1
    n = levels // KC
    NB = L // n
    HB = 2 * Q
    group = 4 if Q % 4 == 0 else 1
    cfg = (KC, Q, M, G, R, KM, V, L, n, W, group)
    vmem = pl.BlockSpec(memory_space=pltpu.VMEM)
    dma = pltpu.SemaphoreType.DMA
    member_control = control.reshape(KM, NB, n * R, W)
    back = pl.pallas_call(
        functools.partial(kernel, cfg),
        out_shape=jax.ShapeDtypeStruct((KM, NB, n * R, W), f32),
        in_specs=[pl.BlockSpec(memory_space=pltpu.HBM)] * 6,
        out_specs=vmem,
        scratch_shapes=[
            pltpu.VMEM((KM, V, NB, n * R, W), jnp.bfloat16),
            pltpu.VMEM((KM, NB, n * R, W), jnp.bfloat16),
            pltpu.VMEM(vertical.shape, vertical.dtype),
            pltpu.VMEM(inverse_var.shape, inverse_var.dtype),
            pltpu.VMEM(obs_code.shape, obs_code.dtype),
            pltpu.VMEM(obs_count.shape, obs_count.dtype),
            pltpu.VMEM((KM, V, NB, n * R, W), f32),
            pltpu.VMEM((KM, NB, n * R, W), f32),
            pltpu.VMEM((KC, R + 4, KM, HB, n, W), f32),
            pltpu.VMEM((KC, 2, Q, V, R, n, W), f32),
            pltpu.VMEM((KC, Q, V, R, n, W), f32),
            pltpu.VMEM((KC, Q, V, R, n, W), f32),
            pltpu.VMEM((KC, Q, V, R, n, W), f32),
            pltpu.VMEM((KC, R + 4, V, n, W), f32),
            pltpu.VMEM((KC, 2, Q, V, R, n, W), f32),
            pltpu.VMEM((KC, R + 4, KM, HB, n, W), f32),
            pltpu.VMEM((2 * R + 4, 8, W), f32),
            pltpu.VMEM((KM, R, NB, n, W), f32),
            dma((6,)),
            dma((KC, 2)), dma((KC, 2)),
            dma((KC,)), dma((KC,)),
            dma((KC, Q)), dma((KC, Q)),
            dma((KC, 2)), dma((KC, 2)),
            dma((KC, Q)), dma((KC, Q)),
            dma((KC, Q)), dma((KC, Q)),
            dma((KC, 2)), dma((KC, 2)),
            dma((1, 2)), dma((1, 2)),
        ],
        compiler_params=pltpu.CompilerParams(collective_id=0, has_side_effects=True),
    )(
        ensemble.reshape(KM, V, NB, n * R, W),
        member_control,
        vertical,
        inverse_var,
        obs_code,
        obs_count,
    )
    return (member_control.astype(f32) + back).reshape(KM, L, R, W)


def solution(mesh):
    return jax.shard_map(
        per_device,
        mesh=mesh,
        in_specs=(
            P("mem", None, None, "grid", None),
            P("mem", None, "grid", None),
            P(),
            P(),
            P("grid", None),
            P("grid", None),
        ),
        out_specs=P("mem", None, "grid", None),
        check_vma=False,
    )
```

```python
import functools
import jax
import jax.numpy as jnp
from jax import lax
from jax.experimental import pallas as pl
from jax.experimental.pallas import tpu as pltpu
from jax.sharding import PartitionSpec as P

diffusion = 0.2
near_weight = 0.75
far_weight = 0.25
f32 = jnp.float32
MESH = pl.DeviceIdType.MESH


def columns(x, by):
    width = x.shape[-1]
    lane = lax.broadcasted_iota(jnp.int32, x.shape, x.ndim - 1)
    moved = pltpu.roll(x, by % width, x.ndim - 1)
    edge = 0 if by == 1 else width - 1
    return jnp.where(lane == edge, 0.0, moved)


def smooth(prev, center, after):
    sides = columns(center, 1) + columns(center, -1)
    return center + diffusion * (after + prev + sides - 4.0 * center)


def smooth_twice(rows, low, high):
    first = [smooth(rows[i - 1], rows[i], rows[i + 1]) for i in range(1, len(rows) - 1)]
    first[0] = first[0] * low
    first[-1] = first[-1] * high
    return [smooth(first[i - 1], first[i], first[i + 1]) for i in range(1, len(first) - 1)]


LAG = (0, 20, 60, 90, 130, 140, 190)


def order_of(chunks, count):
    delay = 35
    at = [(LAG[i] + delay * j, j, i) for j in range(chunks) for i in range(count)]
    return [(i, j) for _, j, i in sorted(at)]


def kernel(cfg, ens_hbm, ctl_hbm, vert_hbm, ivar_hbm, code_hbm, count_hbm, out_ref,
           ens_ref, ctl_ref, vert_ref, ivar_ref, code_ref, count_ref, ensf, ctlf, ext, part, r1, half, r2, share, adj, proj, obs, rnd,
           in_sem, a_s, a_r, b1_s, b1_r, b2_s, b2_r, c_s, c_r, d_s, d_r, p_s, p_r, e_s, e_r, o_s, o_r):
    KC, Q, M, G, R, KM, V, L, n, W, group = cfg
    NB = L // n
    HB = 2 * Q
    factor = (KM * M) ** (-0.5)
    mem = lax.axis_index("mem")
    grid = lax.axis_index("grid")
    core = lax.rem(mem, 2)
    chip = lax.div(mem, 2)
    partner = chip * 2 + (1 - core)
    has_prev = grid > 0
    has_next = grid < G - 1
    before = (mem, jnp.maximum(grid - 1, 0))
    behind = (mem, jnp.minimum(grid + 1, G - 1))
    low = jnp.where(has_prev, 1.0, 0.0).astype(f32)
    high = jnp.where(has_next, 1.0, 0.0).astype(f32)

    def peer(d):
        return (lax.rem(chip + d, Q) * 2 + core, grid)

    barrier = pltpu.get_barrier_semaphore()

    def greet(device):
        pl.semaphore_signal(barrier, inc=1, device_id=device, device_id_type=MESH)

    @pl.when(has_prev)
    def _():
        greet(before)

    @pl.when(has_next)
    def _():
        greet(behind)

    greet((partner, grid))
    for d in range(1, Q):
        greet(peer(d))

    loads = [pltpu.make_async_copy(source, target, in_sem.at[i]) for i, (source, target) in enumerate((
        (ctl_hbm, ctl_ref), (vert_hbm, vert_ref), (code_hbm, code_ref), (count_hbm, count_ref),
        (ivar_hbm, ivar_ref), (ens_hbm, ens_ref)))]
    for load in loads:
        load.start()

    def up_copy(buf, lead, rows, s, r, at):
        return pltpu.make_async_remote_copy(
            src_ref=buf.at[lead + (pl.ds(rows, 2),)], dst_ref=buf.at[lead + (pl.ds(0, 2),)],
            send_sem=s.at[at, 0], recv_sem=r.at[at, 0], device_id=behind, device_id_type=MESH)

    def down_copy(buf, lead, rows, s, r, at):
        return pltpu.make_async_remote_copy(
            src_ref=buf.at[lead + (pl.ds(2, 2),)], dst_ref=buf.at[lead + (pl.ds(rows + 2, 2),)],
            send_sem=s.at[at, 1], recv_sem=r.at[at, 1], device_id=before, device_id_type=MESH)

    def halo_start(*args):
        @pl.when(has_next)
        def _():
            up_copy(*args).start()

        @pl.when(has_prev)
        def _():
            down_copy(*args).start()

    def halo_recv(*args):
        @pl.when(has_prev)
        def _():
            up_copy(*args).wait_recv()

        @pl.when(has_next)
        def _():
            down_copy(*args).wait_recv()

    def halo_sent(*args):
        @pl.when(has_next)
        def _():
            up_copy(*args).wait_send()

        @pl.when(has_prev)
        def _():
            down_copy(*args).wait_send()

    def a_args(j):
        return ext, (j,), R, a_s, a_r, j

    def c_args(j):
        return share, (j,), R, c_s, c_r, j

    def e_args(j):
        return proj, (j,), R, e_s, e_r, j

    o_args = (obs, (), 2 * R, o_s, o_r, 0)

    def core_copy(j):
        return pltpu.make_async_remote_copy(
            src_ref=part.at[j, 1 - core], dst_ref=r1.at[j], send_sem=b1_s.at[j], recv_sem=b1_r.at[j],
            device_id=(partner, grid), device_id_type=MESH)

    def chip_copy(j, d):
        return pltpu.make_async_remote_copy(
            src_ref=half.at[j, lax.rem(chip + d, Q)], dst_ref=r2.at[j, d],
            send_sem=b2_s.at[j, d], recv_sem=b2_r.at[j, d], device_id=peer(d), device_id_type=MESH)

    def gather_copy(j, d):
        return pltpu.make_async_remote_copy(
            src_ref=adj.at[j, core, chip], dst_ref=adj.at[j, core, chip],
            send_sem=d_s.at[j, d], recv_sem=d_r.at[j, d], device_id=peer(d), device_id_type=MESH)

    def pass_copy(j, d):
        source = lax.rem(chip + Q - d, Q)
        return pltpu.make_async_remote_copy(
            src_ref=adj.at[j, core, source], dst_ref=adj.at[j, core, source],
            send_sem=p_s.at[j, d], recv_sem=p_r.at[j, d], device_id=(partner, grid), device_id_type=MESH)

    loads[0].wait()
    loads[1].wait()
    ctlf[...] = ctl_ref[...].astype(f32)
    wide = jnp.concatenate(
        [ctlf[k, :, pl.ds(r, n, stride=R), :].reshape(L, W).astype(jnp.bfloat16)
         for k in range(KM) for r in range(R)], axis=1)
    mixed = jnp.dot(vert_ref[...], wide, preferred_element_type=f32)
    for k in range(KM):
        for r in range(R):
            at = (k * R + r) * W
            ext[:, 2 + r, k] = mixed[:, at:at + W].reshape(KC, HB, n, W)

    def pick():
        i = lax.broadcasted_iota(jnp.int32, (2 * W, 2 * W), 0)
        o = lax.broadcasted_iota(jnp.int32, (2 * W, 2 * W), 1)
        return jnp.where(i == 2 * lax.rem(o, W) + lax.div(o, W), 1.0, 0.0).astype(jnp.bfloat16)

    loads[2].wait()
    loads[3].wait()
    ints = jnp.concatenate([code_ref[...], count_ref[...]], axis=0).astype(f32).astype(jnp.bfloat16)
    apart = jnp.dot(ints, pick(), preferred_element_type=f32)
    for i in range(2 * R):
        for p in range(2):
            obs[2 + i, p:p + 1, :] = apart[i:i + 1, p * W:(p + 1) * W]
            obs[2 + i, 2 + p:3 + p, :] = apart[2 * R + i:2 * R + i + 1, p * W:(p + 1) * W]
        obs[2 + i, 4:8, :] = jnp.zeros((4, W), f32)

    @pl.when(jnp.logical_not(has_prev))
    def _():
        ext[:, 0:2] = jnp.zeros((KC, 2) + ext.shape[2:], f32)
        proj[:, 0:2] = jnp.zeros((KC, 2) + proj.shape[2:], f32)
        share[:, 0:2] = jnp.zeros((KC, 2) + share.shape[2:], f32)
        obs[0:2] = jnp.zeros((2,) + obs.shape[1:], f32)

    @pl.when(jnp.logical_not(has_next))
    def _():
        ext[:, R + 2:R + 4] = jnp.zeros((KC, 2) + ext.shape[2:], f32)
        proj[:, R + 2:R + 4] = jnp.zeros((KC, 2) + proj.shape[2:], f32)
        share[:, R + 2:R + 4] = jnp.zeros((KC, 2) + share.shape[2:], f32)
        obs[2 * R + 2:2 * R + 4] = jnp.zeros((2,) + obs.shape[1:], f32)

    pl.semaphore_wait(barrier, Q + has_prev.astype(jnp.int32) + has_next.astype(jnp.int32))

    for j in range(KC):
        halo_start(*a_args(j))
    halo_start(*o_args)

    loads[4].wait()
    loads[5].wait()
    for k in range(KM):
        def widen(v, _):
            ensf[k, v] = ens_ref[k, v].astype(f32)
            return 0
        lax.fori_loop(0, V, widen, 0)

    halo_recv(*o_args)

    def member(k, v, b0, r):
        return ensf[k, v, pl.ds(b0, group), pl.ds(r, n, stride=R), :]

    def stage_weigh(j):
        halo_recv(*a_args(j))

        def weigh(g, _):
            b0 = g * group
            local = [smooth_twice([ext[j, i, k, pl.ds(b0, group)] for i in range(R + 4)], low, high)
                     for k in range(KM)]
            c, q0 = lax.div(b0, Q), lax.rem(b0, Q)
            for v in range(V):
                for r in range(R):
                    total = member(0, v, j * HB + b0, r) * local[0][r]
                    for k in range(1, KM):
                        total = total + member(k, v, j * HB + b0, r) * local[k][r]
                    part[j, c, pl.ds(q0, group), v, r] = factor * total
            return 0

        lax.fori_loop(0, HB // group, weigh, 0, unroll=HB // group <= 4)
        core_copy(j).start()

    def stage_join(j):
        core_copy(j).wait_recv()

        def join(q, _):
            half[j, q] = part[j, core, q] + r1[j, q]
            return 0

        lax.fori_loop(0, Q, join, 0, unroll=Q <= 4)
        for d in range(1, Q):
            chip_copy(j, d).start()

    def stage_reduce(j):
        total = half[j, chip]
        for d in range(1, Q):
            chip_copy(j, d).wait_recv()
            total = total + r2[j, d]
        for r in range(R):
            share[j, 2 + r] = total[:, r]
        halo_start(*c_args(j))

    def stage_observe(j):
        first_level = (j * HB + core * Q + chip) * n
        hot = (lax.broadcasted_iota(jnp.int32, (n, L), 1)
               == lax.broadcasted_iota(jnp.int32, (n, L), 0) + first_level)
        weights = jnp.stack(
            [jnp.broadcast_to(jnp.sum(jnp.where(hot, ivar_ref[v:v + 1, :], 0.0), axis=1, keepdims=True), (n, W))
             for v in range(V)], axis=0)
        halo_recv(*c_args(j))
        u = [share[j, i] for i in range(R + 4)]
        fine = []
        last = 2 * R + 3
        for i in range(last + 1):
            a = i // 2 + 1
            row = near_weight * u[a] + far_weight * (u[a - 1] if i % 2 == 0 else u[a + 1])
            if i < 2:
                row = row * low
            if i > last - 2:
                row = row * high
            fine.append((near_weight * row + far_weight * columns(row, 1),
                         near_weight * row + far_weight * columns(row, -1)))
        forced, ups, downs = [], [], []
        for i in range(last + 1):
            even_odd, up, down = [], [], []
            right_of = (fine[i][1], columns(fine[i][0], -1)) if 0 < i < last else None
            left_of = (columns(fine[i][1], 1), fine[i][0]) if 0 < i < last else None
            sides = []
            for p in range(2):
                code = obs[i, p:p + 1, :]
                scale = obs[i, 2 + p:3 + p, :] * weights
                m = [jnp.where(code == which, 1.0, 0.0) for which in range(1, 5)]
                diff = fine[i][p]
                if i < last:
                    diff = diff - m[0] * fine[i + 1][p]
                if i > 0:
                    diff = diff - m[1] * fine[i - 1][p]
                if right_of is not None:
                    diff = diff - m[2] * right_of[p] - m[3] * left_of[p]
                force = scale * diff
                even_odd.append(force)
                up.append(m[0] * force)
                down.append(m[1] * force)
                sides.append((m[2] * force, m[3] * force))
            ups.append(up)
            downs.append(down)
            if 0 < i < last:
                even = even_odd[0] - columns(sides[1][0], 1) - sides[1][1]
                odd = even_odd[1] - sides[0][0] - columns(sides[0][1], -1)
                forced.append((even, odd))
            else:
                forced.append(None)
        back = [None] * (last + 1)
        for i in range(1, last):
            pair = [forced[i][p] - ups[i - 1][p] - downs[i + 1][p] for p in range(2)]
            if i == 1:
                pair = [x * low for x in pair]
            if i == last - 1:
                pair = [x * high for x in pair]
            back[i] = pair
        for r in range(R):
            i = 2 * r + 2
            even, odd = [near_weight * (back[i][p] + back[i + 1][p]) + far_weight * (back[i - 1][p] + back[i + 2][p])
                         for p in range(2)]
            row = near_weight * (even + odd) + far_weight * (columns(odd, 1) + columns(even, -1))
            adj[j, core, chip, :, r] = row
        for d in range(1, Q):
            gather_copy(j, d).start()
        pass_copy(j, 0).start()

    def stage_forward(j):
        for d in range(1, Q):
            gather_copy(j, d).wait_recv()
            pass_copy(j, d).start()

    def arrived(j, d):
        source = lax.rem(chip + Q - d, Q)
        return pltpu.make_async_remote_copy(
            src_ref=adj.at[j, 1 - core, source], dst_ref=adj.at[j, 1 - core, source],
            send_sem=p_s.at[j, d], recv_sem=p_r.at[j, d], device_id=(partner, grid), device_id_type=MESH)

    def stage_project(j):
        for d in range(Q):
            arrived(j, d).wait_recv()

        def project(g, _):
            b0 = g * group
            c, q0 = lax.div(b0, Q), lax.rem(b0, Q)
            for r in range(R):
                fields = [adj[j, c, pl.ds(q0, group), v, r] for v in range(V)]
                for k in range(KM):
                    total = member(k, 0, j * HB + b0, r) * fields[0]
                    for v in range(1, V):
                        total = total + member(k, v, j * HB + b0, r) * fields[v]
                    proj[j, 2 + r, k, pl.ds(b0, group)] = factor * total
            return 0

        lax.fori_loop(0, HB // group, project, 0, unroll=HB // group <= 4)
        halo_start(*e_args(j))

    def stage_settle(j):
        halo_recv(*e_args(j))

        def settle(g, _):
            b0 = g * group
            for k in range(KM):
                rows = smooth_twice([proj[j, i, k, pl.ds(b0, group)] for i in range(R + 4)], low, high)
                for r in range(R):
                    rnd[k, r, pl.ds(j * HB + b0, group)] = rows[r]
            return 0

        lax.fori_loop(0, HB // group, settle, 0, unroll=HB // group <= 4)

    stages = (stage_weigh, stage_join, stage_reduce, stage_observe, stage_forward, stage_project, stage_settle)
    for index, j in order_of(KC, len(stages)):
        stages[index](j)

    wide = jnp.concatenate(
        [rnd[k, r].reshape(L, W).astype(jnp.bfloat16) for k in range(KM) for r in range(R)], axis=1)
    product = lax.dot_general(vert_ref[...], wide, (((0,), (0,)), ((), ())), preferred_element_type=f32)
    for k in range(KM):
        for r in range(R):
            at = (k * R + r) * W
            out_ref[k, :, pl.ds(r, n, stride=R), :] = product[:, at:at + W].reshape(NB, n, W)

    halo_sent(*o_args)
    for j in range(KC):
        halo_sent(*a_args(j))
        core_copy(j).wait_send()
        for d in range(1, Q):
            chip_copy(j, d).wait_send()
            gather_copy(j, d).wait_send()
        halo_sent(*c_args(j))
        for d in range(Q):
            pass_copy(j, d).wait_send()
        halo_sent(*e_args(j))


def per_device(ensemble, control, vertical, inverse_var, obs_code, obs_count):
    KM, V, L, R, W = ensemble.shape
    M = lax.axis_size("mem")
    G = lax.axis_size("grid")
    Q = M // 2
    levels = L // M
    KC = 2 if levels % 16 == 0 else 1
    n = levels // KC
    NB = L // n
    HB = 2 * Q
    group = 4 if Q % 4 == 0 else 1
    cfg = (KC, Q, M, G, R, KM, V, L, n, W, group)
    vmem = pl.BlockSpec(memory_space=pltpu.VMEM)
    dma = pltpu.SemaphoreType.DMA
    member_control = control.reshape(KM, NB, n * R, W)
    back = pl.pallas_call(
        functools.partial(kernel, cfg),
        out_shape=jax.ShapeDtypeStruct((KM, NB, n * R, W), f32),
        in_specs=[pl.BlockSpec(memory_space=pltpu.HBM)] * 6,
        out_specs=vmem,
        scratch_shapes=[
            pltpu.VMEM((KM, V, NB, n * R, W), jnp.bfloat16),
            pltpu.VMEM((KM, NB, n * R, W), jnp.bfloat16),
            pltpu.VMEM(vertical.shape, vertical.dtype),
            pltpu.VMEM(inverse_var.shape, inverse_var.dtype),
            pltpu.VMEM(obs_code.shape, obs_code.dtype),
            pltpu.VMEM(obs_count.shape, obs_count.dtype),
            pltpu.VMEM((KM, V, NB, n * R, W), f32),
            pltpu.VMEM((KM, NB, n * R, W), f32),
            pltpu.VMEM((KC, R + 4, KM, HB, n, W), f32),
            pltpu.VMEM((KC, 2, Q, V, R, n, W), f32),
            pltpu.VMEM((KC, Q, V, R, n, W), f32),
            pltpu.VMEM((KC, Q, V, R, n, W), f32),
            pltpu.VMEM((KC, Q, V, R, n, W), f32),
            pltpu.VMEM((KC, R + 4, V, n, W), f32),
            pltpu.VMEM((KC, 2, Q, V, R, n, W), f32),
            pltpu.VMEM((KC, R + 4, KM, HB, n, W), f32),
            pltpu.VMEM((2 * R + 4, 8, W), f32),
            pltpu.VMEM((KM, R, NB, n, W), f32),
            dma((6,)),
            dma((KC, 2)), dma((KC, 2)),
            dma((KC,)), dma((KC,)),
            dma((KC, Q)), dma((KC, Q)),
            dma((KC, 2)), dma((KC, 2)),
            dma((KC, Q)), dma((KC, Q)),
            dma((KC, Q)), dma((KC, Q)),
            dma((KC, 2)), dma((KC, 2)),
            dma((1, 2)), dma((1, 2)),
        ],
        compiler_params=pltpu.CompilerParams(collective_id=0, has_side_effects=True),
    )(
        ensemble.reshape(KM, V, NB, n * R, W),
        member_control,
        vertical,
        inverse_var,
        obs_code,
        obs_count,
    )
    return (member_control.astype(f32) + back).reshape(KM, L, R, W)


def solution(mesh):
    return jax.shard_map(
        per_device,
        mesh=mesh,
        in_specs=(
            P("mem", None, None, "grid", None),
            P("mem", None, "grid", None),
            P(),
            P(),
            P("grid", None),
            P("grid", None),
        ),
        out_specs=P("mem", None, "grid", None),
        check_vma=False,
    )
```
